256 devices in a mesh: rep: 2 (over z_hi), fsdp: 32 (over y, x, core), tp: 4 (over z_lo).
Axes of the slice: x: 4, y: 4, z: 8 (z_hi: 2, z_lo: 4; z = z_hi * 4 + z_lo), core: 2. Of those that a mesh axis runs over, the one named last changes fastest.
Arguments:
- delta_out: float32 [2, 8, 1792, 1792], P('rep', None, 'tp', 'fsdp'), may hold values from -6 to 6
- delta_down: float32 [2, 8, 4864, 1792], P('rep', None, 'tp', 'fsdp'), may hold values from -6 to 6
- basis: float32 [1792, 64], replicated, may hold values from -0.125 to 0.125
- anchor_out: float32 [8, 4, 448, 1792], P('rep', 'tp', 'fsdp'), may hold values from -6 to 6
- anchor_down: float32 [8, 4, 1216, 1792], P('rep', 'tp', 'fsdp'), may hold values from -6 to 6
- moment_out: float32 [8, 4, 448, 1792], P('rep', 'tp', 'fsdp'), may hold values from -3 to 3
- moment_down: float32 [8, 4, 1216, 1792], P('rep', 'tp', 'fsdp'), may hold values from -3 to 3
Outputs:
- weights_out: bfloat16 [8, 1792, 1792], P(None, 'tp', 'fsdp')
- weights_down: bfloat16 [8, 4864, 1792], P(None, 'tp', 'fsdp')
- anchor_out_new: float32 [8, 4, 448, 1792], P('rep', 'tp', 'fsdp')
- anchor_down_new: float32 [8, 4, 1216, 1792], P('rep', 'tp', 'fsdp')
- moment_out_new: float32 [8, 4, 448, 1792], P('rep', 'tp', 'fsdp')
- moment_down_new: float32 [8, 4, 1216, 1792], P('rep', 'tp', 'fsdp')
The draws below stay inside these ranges and needn't reach their ends.
All inputs are finite; a program needn't handle non-finite values.
Results may differ from the reference program's by a relative error of at most 0.0055.
Values may be sent and summed in bfloat16 or wider, within the bound.
A program may use at most 64 MiB of HBM per device.

```python
import jax
import jax.numpy as jnp
from jax import lax

D = 1792
FF = 4864
RANK = 64
LAYERS = 8
REP = 2
N_TP = 4


def block_scale(rng, extent, shards, least, top_value):
    gain = 1.0
    for axis_at, parts in shards:
        draws = jax.random.uniform(jax.random.fold_in(jax.random.fold_in(rng, 6), axis_at), (parts,), jnp.float32, least / len(shards), top_value / len(shards))
        gain = gain * jnp.repeat(jnp.exp(draws), extent[axis_at] // parts).reshape((-1,) + (1,) * (len(extent) - 1 - axis_at))
    return gain


def noise(key, extent, scale, limit, pieces=(), held_as=jnp.bfloat16):
    result = jax.random.normal(key, extent, jnp.float32) * scale
    if len(pieces) > 0:
        result = block_scale(key, extent, pieces, -0.22, 0.18) * result
    return jnp.clip(result, min=-limit, max=limit).astype(held_as)


def setup_inputs(seed: int = 0) -> dict:
    arg_keys = jax.random.split(jax.random.key(seed), 8)
    return {
        "delta_out": noise(arg_keys[0], (REP, LAYERS, D, D), 1.0, 6.0, ((0, 2), (2, 4), (3, 32)), jnp.float32),
        "delta_down": noise(arg_keys[1], (REP, LAYERS, FF, D), 1.0, 6.0, ((0, 2), (2, 4), (3, 32)), jnp.float32),
        "basis": noise(arg_keys[2], (D, RANK), D ** -0.5, 0.125, (), jnp.float32),
        "anchor_out": noise(arg_keys[3], (LAYERS, N_TP, D // N_TP, D), 1.0, 6.0, ((0, 2), (1, 4), (2, 32)), jnp.float32),
        "anchor_down": noise(arg_keys[4], (LAYERS, N_TP, FF // N_TP, D), 1.0, 6.0, ((0, 2), (1, 4), (2, 32)), jnp.float32),
        "moment_out": noise(arg_keys[5], (LAYERS, N_TP, D // N_TP, D), 0.5, 3.0, ((0, 2), (1, 4), (2, 32)), jnp.float32),
        "moment_down": noise(arg_keys[6], (LAYERS, N_TP, FF // N_TP, D), 0.5, 3.0, ((0, 2), (1, 4), (2, 32)), jnp.float32),
    }


outer_rate = 0.7
nesterov_decay = 0.9


def update_matrix(delta, basis, anchor, moment):
    groups = delta.shape[0]
    coef = jnp.einsum("rlij,jk->lik", delta, basis, precision=lax.Precision.HIGHEST) / groups
    grad = jnp.einsum("lik,jk->lij", coef, basis, precision=lax.Precision.HIGHEST)
    previous = anchor.reshape(grad.shape)
    velocity = moment.reshape(grad.shape)
    moment_new = nesterov_decay * velocity + grad
    anchor_new = previous - outer_rate * (grad + nesterov_decay * moment_new)
    weights = anchor_new.astype(jnp.bfloat16)
    return weights, anchor_new.reshape(anchor.shape), moment_new.reshape(moment.shape)


def reference(delta_out, delta_down, basis, anchor_out, anchor_down, moment_out, moment_down):
    weights_out, anchor_out_new, moment_out_new = update_matrix(delta_out, basis, anchor_out, moment_out)
    weights_down, anchor_down_new, moment_down_new = update_matrix(delta_down, basis, anchor_down, moment_down)
    return (weights_out, weights_down, anchor_out_new, anchor_down_new, moment_out_new, moment_down_new)
```

```python
import jax
import jax.numpy as jnp
from jax import lax
from jax.experimental import pallas as pl
from jax.experimental.pallas import tpu as pltpu
from jax.sharding import PartitionSpec as P

MESH = pl.DeviceIdType.MESH
outer_rate = 0.7
nesterov_decay = 0.9
base_decay = outer_rate * nesterov_decay * nesterov_decay
grad_gain = outer_rate * (1.0 + nesterov_decay)

LANES = 128
COLS = 56
ROWS_OUT, ROWS_DOWN = 448, 1216
OWN_OUT, OWN_DOWN = 14, 38
WIDE_OUT, WIDE_DOWN = 512, 1280
WIDE = WIDE_OUT + WIDE_DOWN
MSG = 2 * (OWN_OUT + OWN_DOWN)
CHUNKS = 14
N_FSDP = 32
CHIPS = 16
PIECE = 16
F32, BF16 = jnp.float32, jnp.bfloat16


def column_window(load_chunk, index):
    first = (7 * index) // 16
    offset = COLS * index - LANES * first
    second = jnp.minimum(first + 1, CHUNKS - 1)
    return load_chunk(first), load_chunk(second), offset


def own_basis(basis_ref, f):
    low, high, offset = column_window(
        lambda k: basis_ref[:, pl.ds(pl.multiple_of(k * LANES, LANES), LANES)], f
    )
    lane = lax.broadcasted_iota(jnp.int32, low.shape, 1)
    window = jnp.where(lane >= offset, low, high)
    window = pltpu.roll(window, lax.rem(LANES - offset, LANES), 1)
    return jnp.where(lane < COLS, window, 0.0)


def split(x):
    high = x.astype(BF16)
    return high, (x - high.astype(F32)).astype(BF16)


def exchange_kernel(
    dout_hbm, ddown_hbm, basis_hbm, aout_hbm, adown_hbm, mout_hbm, mdown_hbm,
    rows_hbm, coef_hbm,
    dout, ddown, basis, aout, adown, mout, mdown,
    stack, part, part16, cross, half, gathered, mine, theirs, final, base, src,
    in_sem, local_sem, base_send, base_recv, core_send, core_recv, rs_send, rs_recv,
    rep_send, rep_recv, ag_send, ag_recv, fw_send, fw_recv,
):
    r = lax.axis_index("rep")
    f = lax.axis_index("fsdp")
    t = lax.axis_index("tp")
    chip, core = f // 2, lax.rem(f, 2)
    other = 1 - core
    me = r * N_FSDP + f

    loads = [
        pltpu.make_async_copy(a, b, in_sem.at[i])
        for i, (a, b) in enumerate(
            ((basis_hbm, basis), (dout_hbm, dout), (ddown_hbm, ddown), (aout_hbm, aout),
             (mout_hbm, mout), (adown_hbm, adown), (mdown_hbm, mdown))
        )
    ]
    for copy in loads:
        copy.start()

    barrier = pltpu.get_barrier_semaphore()

    def greet(i, carry):
        peer = lax.rem(me + i, 2 * N_FSDP)
        pl.semaphore_signal(
            barrier, inc=1, device_id=(peer // N_FSDP, lax.rem(peer, N_FSDP), t), device_id_type=MESH
        )
        return carry

    lax.fori_loop(1, 2 * N_FSDP, greet, 0)

    stack[...] = jnp.zeros_like(stack)
    for copy in loads[:3]:
        copy.wait()
    high, low = split(own_basis(basis, f))
    high2 = high.astype(F32)
    left = jnp.concatenate([(high2 + pltpu.roll(high2, 64, 1)).astype(BF16), low], axis=1)

    def project(l, carry):
        for ref, lanes in ((dout, pl.ds(0, ROWS_OUT)), (ddown, pl.ds(WIDE_OUT, ROWS_DOWN))):
            hi, lo = split(ref[l])
            stack[0:COLS, lanes] = hi
            stack[64 : 64 + COLS, lanes] = lo
            stack[128 : 128 + COLS, lanes] = hi
        coef = jnp.dot(left, stack[...], preferred_element_type=F32)
        for a in range(2):
            for b in range(2):
                rows = coef[PIECE * (2 * a + b) : PIECE * (2 * a + b + 1)]
                part[2 * l + a, b] = rows
                part16[2 * l + a, b] = rows.astype(BF16)
        return carry

    lax.fori_loop(0, 8, project, 0)

    for copy in loads[3:]:
        copy.wait()

    def combine(c, carry):
        for h in range(2):
            for a, m, count, at in ((aout, mout, 28, 0), (adown, mdown, 76, 28)):
                rows = pl.ds(c + CHUNKS * count * h, count, stride=CHUNKS)
                base[h, c, at : at + count, :] = a[rows, :] - base_decay * m[rows, :]
        return carry

    lax.fori_loop(0, CHUNKS, combine, 0)

    def pack(j, carry):
        low0, high0, offset = column_window(lambda k: base[0, k], j)
        low1, high1, _ = column_window(lambda k: base[1, k], j)
        lane = lax.broadcasted_iota(jnp.int32, low0.shape, 1)
        first = pltpu.roll(jnp.where(lane >= offset, low0, high0), lax.rem(LANES - offset, LANES), 1)
        second = pltpu.roll(jnp.where(lane >= offset, low1, high1), lax.rem(LANES + 64 - offset, LANES), 1)
        src[j] = jnp.where(lane < 64, first, second).astype(BF16)
        return carry

    lax.fori_loop(0, N_FSDP, pack, 0)

    pl.semaphore_wait(barrier, 2 * N_FSDP - 1)

    partner_core = (r, 2 * chip + other, t)
    core_copy = pltpu.make_async_remote_copy(
        part16.at[:, other], cross, core_send, core_recv, device_id=partner_core, device_id_type=MESH
    )
    core_copy.start()

    def send_across(i, carry):
        j = lax.rem(f + i, N_FSDP)
        pltpu.make_async_remote_copy(
            src.at[j], rows_hbm.at[r, f], base_send.at[0], base_recv.at[0],
            device_id=(1 - r, j, t), device_id_type=MESH,
        ).start()
        return carry

    def send_within(i, carry):
        j = lax.rem(f + i, N_FSDP)
        pltpu.make_async_remote_copy(
            src.at[j], rows_hbm.at[r, f], base_send.at[1], base_recv.at[1],
            device_id=(r, j, t), device_id_type=MESH,
        ).start()
        return carry

    lax.fori_loop(0, 16, send_across, 0)
    own_rows = pltpu.make_async_copy(src.at[f], rows_hbm.at[r, f], local_sem.at[0])
    own_rows.start()

    core_copy.wait_recv()

    def halve(p, carry):
        half[p] = (part[p, core] + cross[p].astype(F32)).astype(BF16)
        return carry

    lax.fori_loop(0, CHIPS, halve, 0)
    gathered[chip] = half[chip]

    def send_half(i, carry):
        p = lax.rem(chip + i, CHIPS)
        pltpu.make_async_remote_copy(
            half.at[p], gathered.at[chip], rs_send, rs_recv,
            device_id=(r, 2 * p + core, t), device_id_type=MESH,
        ).start()
        return carry

    lax.fori_loop(1, CHIPS, send_half, 0)
    lax.fori_loop(1, N_FSDP, send_within, 0)

    rs_wait = pltpu.make_async_remote_copy(
        half.at[pl.ds(0, CHIPS - 1)], gathered.at[pl.ds(0, CHIPS - 1)], rs_send, rs_recv,
        device_id=partner_core, device_id_type=MESH,
    )
    rs_wait.wait_recv()
    total = gathered[0].astype(F32)
    for p in range(1, CHIPS):
        total = total + gathered[p].astype(F32)
    mine[...] = total.astype(BF16)
    rep_copy = pltpu.make_async_remote_copy(
        mine, theirs, rep_send, rep_recv, device_id=(1 - r, f, t), device_id_type=MESH
    )
    rep_copy.start()
    lax.fori_loop(16, N_FSDP, send_across, 0)
    rep_copy.wait_recv()
    final[...] = (0.5 * (mine[...].astype(F32) + theirs[...].astype(F32))).astype(BF16)

    def send_final(i, carry):
        p = lax.rem(chip + i, CHIPS)
        pltpu.make_async_remote_copy(
            final, coef_hbm.at[chip, core], ag_send, ag_recv.at[chip],
            device_id=(r, 2 * p + core, t), device_id_type=MESH,
        ).start()
        return carry

    pltpu.make_async_remote_copy(
        final, coef_hbm.at[chip, core], ag_send, fw_recv, device_id=partner_core, device_id_type=MESH
    ).start()
    lax.fori_loop(1, CHIPS, send_final, 0)
    own_coef = pltpu.make_async_copy(final, coef_hbm.at[chip, core], local_sem.at[1])
    own_coef.start()

    def forward(i, carry):
        p = lax.rem(chip + CHIPS - i, CHIPS)
        pltpu.make_async_remote_copy(
            final, coef_hbm.at[p, core], ag_send, ag_recv.at[p], device_id=partner_core, device_id_type=MESH
        ).wait_recv()
        pltpu.make_async_remote_copy(
            coef_hbm.at[p, core], coef_hbm.at[p, core], fw_send, fw_recv,
            device_id=partner_core, device_id_type=MESH,
        ).start()
        return carry

    lax.fori_loop(1, CHIPS, forward, 0)

    own_rows.wait()
    own_coef.wait()
    core_copy.wait_send()
    rs_wait.wait_send()
    rep_copy.wait_send()

    def settle(sent, landed, send, recv):
        copy = pltpu.make_async_remote_copy(
            sent, landed, send, recv, device_id=partner_core, device_id_type=MESH
        )
        copy.wait_send()
        copy.wait_recv()

    settle(src, rows_hbm.at[1 - r], base_send.at[0], base_recv.at[0])
    most = pl.ds(0, N_FSDP - 1)
    settle(src.at[most], rows_hbm.at[r, most], base_send.at[1], base_recv.at[1])
    pltpu.make_async_remote_copy(
        half, half, ag_send, fw_recv, device_id=partner_core, device_id_type=MESH
    ).wait_send()
    pltpu.make_async_remote_copy(
        half.at[pl.ds(0, CHIPS - 1)], half.at[pl.ds(0, CHIPS - 1)], fw_send, fw_recv,
        device_id=partner_core, device_id_type=MESH,
    ).wait_send()
    pltpu.make_async_remote_copy(
        half, coef_hbm.at[:, other], fw_send, fw_recv, device_id=partner_core, device_id_type=MESH
    ).wait_recv()


def exchange(dout, ddown, basis, aout, adown, mout, mdown):
    any_spec = pl.BlockSpec(memory_space=pl.ANY)
    sem = pltpu.SemaphoreType.DMA
    return pl.pallas_call(
        exchange_kernel,
        name="exchange",
        out_shape=(
            jax.ShapeDtypeStruct((2, N_FSDP, MSG, LANES), BF16),
            jax.ShapeDtypeStruct((CHIPS, 2, PIECE, WIDE), BF16),
        ),
        in_specs=[any_spec] * 7,
        out_specs=(any_spec, any_spec),
        scratch_shapes=[
            pltpu.VMEM(dout.shape, F32),
            pltpu.VMEM(ddown.shape, F32),
            pltpu.VMEM(basis.shape, F32),
            pltpu.VMEM(aout.shape, F32),
            pltpu.VMEM(adown.shape, F32),
            pltpu.VMEM(mout.shape, F32),
            pltpu.VMEM(mdown.shape, F32),
            pltpu.VMEM((256, WIDE), BF16),
            pltpu.VMEM((CHIPS, 2, PIECE, WIDE), F32),
            pltpu.VMEM((CHIPS, 2, PIECE, WIDE), BF16),
            pltpu.VMEM((CHIPS, PIECE, WIDE), BF16),
            pltpu.VMEM((CHIPS, PIECE, WIDE), BF16),
            pltpu.VMEM((CHIPS, PIECE, WIDE), BF16),
            pltpu.VMEM((PIECE, WIDE), BF16),
            pltpu.VMEM((PIECE, WIDE), BF16),
            pltpu.VMEM((PIECE, WIDE), BF16),
            pltpu.VMEM((2, CHUNKS, MSG, LANES), F32),
            pltpu.VMEM((N_FSDP, MSG, LANES), BF16),
            sem((7,)), sem((2,)), sem((2,)), sem((2,)), sem, sem, sem, sem,
            sem, sem, sem, sem((CHIPS,)), sem, sem,
        ],
        compiler_params=pltpu.CompilerParams(
            collective_id=0, has_side_effects=True, vmem_limit_bytes=56 * 1024 * 1024
        ),
    )(dout, ddown, basis, aout, adown, mout, mdown)


TN = (((0,), (0,)), ((), ()))
NT = (((1,), (1,)), ((), ()))


def placement(first, count, height, shift, own, tile):
    shape = (count, height, 2 * LANES)
    source = lax.broadcasted_iota(jnp.int32, shape, 0) + first
    lane = lax.broadcasted_iota(jnp.int32, shape, 2)
    second = lane >= LANES
    row = jnp.where(second, lane - LANES, lane) + LANES * tile
    at = lax.broadcasted_iota(jnp.int32, shape, 1) - shift - jnp.where(second, own, 0)
    hit = (row - own * source == at) & (at >= 0) & (at < own)
    return jnp.where(hit, 1.0, 0.0).astype(BF16).reshape(count * height, 2 * LANES)


def finish_kernel(
    place, rows, coef, basis, aout, adown, mout, mdown,
    wout, wdown, aout_new, adown_new, mout_new, mdown_new, grad,
):
    r, f = place[0], place[1]
    high, low = split(own_basis(basis, f))
    left = jnp.concatenate([high, low], axis=0)

    def project(l, carry):
        c = coef[l]
        g = lax.dot_general(left, jnp.concatenate([c, c], axis=0), TN, preferred_element_type=F32)
        grad[l] = grad_gain * g[:COLS]
        return carry

    lax.fori_loop(0, 8, project, 0)

    for out, own, count, height, begin, shift, total, lane0 in (
        (wout, OWN_OUT, 10, 32, 0, 0, ROWS_OUT, 0),
        (wdown, OWN_DOWN, 5, 80, 24, 4, ROWS_DOWN, WIDE_OUT),
    ):
        for tile in range((total + LANES - 1) // LANES):
            first = min((LANES * tile) // own, N_FSDP - count)
            pick = placement(first, count, height, shift, own, tile)
            width = min(LANES, total - LANES * tile)
            for g in range(2):
                got = rows[g, first : first + count, begin : begin + height, :].reshape(count * height, LANES)
                placed = lax.dot_general(got, pick, TN, preferred_element_type=F32)
                for h in range(2):
                    for b in range(2):
                        l = 4 * g + 2 * h + b
                        lanes = pl.ds(lane0 + LANES * tile, width)
                        value = placed[64 * h : 64 * h + COLS, LANES * b : LANES * b + width] - grad[l, :, lanes]
                        out[l, :, pl.ds(LANES * tile, width)] = value.astype(BF16)

    bhigh, blow = split(basis[...])
    for a, m, a_new, m_new, own, lane0, wide in (
        (aout, mout, aout_new, mout_new, OWN_OUT, 0, WIDE_OUT),
        (adown, mdown, adown_new, mdown_new, OWN_DOWN, WIDE_OUT, WIDE_DOWN),
    ):
        n = 4 * own
        picked = jnp.zeros((n, 64), F32)
        for l in range(4):
            row = lax.broadcasted_iota(jnp.int32, (n, wide), 0) - own * l
            lane = lax.broadcasted_iota(jnp.int32, (n, wide), 1)
            hit = (lane - own * f == row) & (row >= 0) & (row < own)
            one = jnp.where(hit, 1.0, 0.0).astype(BF16)
            picked = picked + lax.dot_general(
                one, coef[4 * r + l, :, pl.ds(lane0, wide)], NT, preferred_element_type=F32
            )
        picked = picked.astype(BF16)
        step = jnp.dot(picked, bhigh, preferred_element_type=F32) + jnp.dot(
            picked, blow, preferred_element_type=F32
        )
        for c in range(CHUNKS):
            at = pl.ds(c, n, stride=CHUNKS)
            g = step[:, LANES * c : LANES * (c + 1)]
            moment = nesterov_decay * m[at, :] + g
            m_new[at, :] = moment
            a_new[at, :] = a[at, :] - outer_rate * (g + nesterov_decay * moment)


def finish(place, rows, coef, basis, aout, adown, mout, mdown):
    vmem = pl.BlockSpec(memory_space=pltpu.VMEM)
    return pl.pallas_call(
        finish_kernel,
        name="finish",
        out_shape=(
            jax.ShapeDtypeStruct((8, COLS, ROWS_OUT), BF16),
            jax.ShapeDtypeStruct((8, COLS, ROWS_DOWN), BF16),
            jax.ShapeDtypeStruct(aout.shape, F32),
            jax.ShapeDtypeStruct(adown.shape, F32),
            jax.ShapeDtypeStruct(aout.shape, F32),
            jax.ShapeDtypeStruct(adown.shape, F32),
        ),
        in_specs=[pl.BlockSpec(memory_space=pltpu.SMEM)] + [vmem] * 7,
        out_specs=(vmem,) * 6,
        scratch_shapes=[pltpu.VMEM((8, COLS, WIDE), F32)],
        compiler_params=pltpu.CompilerParams(vmem_limit_bytes=56 * 1024 * 1024),
    )(place, rows, coef, basis, aout, adown, mout, mdown)


def per_device(delta_out, delta_down, basis, anchor_out, anchor_down, moment_out, moment_down):
    dout = jnp.transpose(delta_out[0], (0, 2, 1))
    ddown = jnp.transpose(delta_down[0], (0, 2, 1))
    basis_t = basis.T
    flat = [x.reshape(-1, LANES) for x in (anchor_out, anchor_down, moment_out, moment_down)]
    rows, coef = exchange(dout, ddown, basis_t, *flat)
    place = jnp.stack([lax.axis_index("rep"), lax.axis_index("fsdp")]).astype(jnp.int32)
    wout, wdown, aout, adown, mout, mdown = finish(
        place, rows, coef.reshape(8, 64, WIDE), basis_t, *flat
    )
    return (
        jnp.transpose(wout, (0, 2, 1)),
        jnp.transpose(wdown, (0, 2, 1)),
        aout.reshape(anchor_out.shape),
        adown.reshape(anchor_down.shape),
        mout.reshape(moment_out.shape),
        mdown.reshape(moment_down.shape),
    )


def solution(mesh):
    return jax.shard_map(
        per_device,
        mesh=mesh,
        in_specs=(
            P("rep", None, "tp", "fsdp"),
            P("rep", None, "tp", "fsdp"),
            P(),
            P("rep", "tp", "fsdp", None),
            P("rep", "tp", "fsdp", None),
            P("rep", "tp", "fsdp", None),
            P("rep", "tp", "fsdp", None),
        ),
        out_specs=(
            P(None, "tp", "fsdp"),
            P(None, "tp", "fsdp"),
            P("rep", "tp", "fsdp", None),
            P("rep", "tp", "fsdp", None),
            P("rep", "tp", "fsdp", None),
            P("rep", "tp", "fsdp", None),
        ),
        check_vma=False,
    )
```

```python
import jax
import jax.numpy as jnp
from jax import lax
from jax.experimental import pallas as pl
from jax.experimental.pallas import tpu as pltpu
from jax.sharding import PartitionSpec as P

MESH = pl.DeviceIdType.MESH
outer_rate = 0.7
nesterov_decay = 0.9
base_decay = outer_rate * nesterov_decay * nesterov_decay
grad_gain = outer_rate * (1.0 + nesterov_decay)

LANES = 128
COLS = 56
ROWS_OUT, ROWS_DOWN = 448, 1216
OWN_OUT, OWN_DOWN = 14, 38
WIDE_OUT, WIDE_DOWN = 512, 1280
WIDE = WIDE_OUT + WIDE_DOWN
MSG = 2 * (OWN_OUT + OWN_DOWN)
CHUNKS = 14
N_FSDP = 32
CHIPS = 16
PIECE = 16
FIRST = 16
F32, BF16 = jnp.float32, jnp.bfloat16


def column_window(load_chunk, index):
    first = (7 * index) // 16
    offset = COLS * index - LANES * first
    second = jnp.minimum(first + 1, CHUNKS - 1)
    return load_chunk(first), load_chunk(second), offset


def own_basis(basis_ref, f):
    low, high, offset = column_window(
        lambda k: basis_ref[:, pl.ds(pl.multiple_of(k * LANES, LANES), LANES)], f
    )
    lane = lax.broadcasted_iota(jnp.int32, low.shape, 1)
    window = jnp.where(lane >= offset, low, high)
    window = pltpu.roll(window, lax.rem(LANES - offset, LANES), 1)
    return jnp.where(lane < COLS, window, 0.0)


def split(x):
    high = x.astype(BF16)
    return high, (x - high.astype(F32)).astype(BF16)


def exchange_kernel(
    dout_hbm, ddown_hbm, basis_hbm, aout_hbm, adown_hbm, mout_hbm, mdown_hbm,
    rows_hbm, coef_hbm,
    dout, ddown, basis, aout, adown, mout, mdown,
    stack, part, part16, cross, half, gathered, mine, theirs, final, base, src,
    in_sem, local_sem, base_send, base_recv, across_send, across_recv, core_send, core_recv, rs_send, rs_recv,
    rep_send, rep_recv, ag_send, ag_recv, fw_send, fw_recv,
):
    r = lax.axis_index("rep")
    f = lax.axis_index("fsdp")
    t = lax.axis_index("tp")
    chip, core = f // 2, lax.rem(f, 2)
    other = 1 - core

    loads = [
        pltpu.make_async_copy(a, b, in_sem.at[i])
        for i, (a, b) in enumerate(
            ((aout_hbm, aout), (mout_hbm, mout), (adown_hbm, adown), (mdown_hbm, mdown),
             (basis_hbm, basis), (dout_hbm, dout), (ddown_hbm, ddown))
        )
    ]
    for copy in loads:
        copy.start()

    barrier = pltpu.get_barrier_semaphore()

    def greet(i, carry):
        pl.semaphore_signal(
            barrier, inc=1, device_id=(r, lax.rem(f + i, N_FSDP), t), device_id_type=MESH
        )
        return carry

    lax.fori_loop(1, N_FSDP, greet, 0)
    pl.semaphore_signal(barrier, inc=1, device_id=(1 - r, f, t), device_id_type=MESH)

    for copy in loads[:4]:
        copy.wait()

    def combine(c, carry):
        for h in range(2):
            for a, m, count, at in ((aout, mout, 28, 0), (adown, mdown, 76, 28)):
                rows = pl.ds(c + CHUNKS * count * h, count, stride=CHUNKS)
                base[h, c, at : at + count, :] = a[rows, :] - base_decay * m[rows, :]
        return carry

    lax.fori_loop(0, CHUNKS, combine, 0)

    def pack(j, carry):
        low0, high0, offset = column_window(lambda k: base[0, k], j)
        low1, high1, _ = column_window(lambda k: base[1, k], j)
        lane = lax.broadcasted_iota(jnp.int32, low0.shape, 1)
        first = pltpu.roll(jnp.where(lane >= offset, low0, high0), lax.rem(LANES - offset, LANES), 1)
        second = pltpu.roll(jnp.where(lane >= offset, low1, high1), lax.rem(LANES + 64 - offset, LANES), 1)
        src[j] = jnp.where(lane < 64, first, second).astype(BF16)
        return carry

    lax.fori_loop(0, N_FSDP, pack, 0)

    pl.semaphore_wait(barrier, N_FSDP)

    def send_within(i, carry):
        j = lax.rem(f + i, N_FSDP)
        pltpu.make_async_remote_copy(
            src.at[j], rows_hbm.at[r, f], base_send, base_recv.at[f],
            device_id=(r, j, t), device_id_type=MESH,
        ).start()
        return carry

    def send_across(i, carry):
        p = lax.rem(f + N_FSDP - i, N_FSDP)
        pltpu.make_async_remote_copy(
            src.at[p], rows_hbm.at[r, p], base_send, base_recv.at[p],
            device_id=(1 - r, f, t), device_id_type=MESH,
        ).wait_recv()
        pltpu.make_async_remote_copy(
            rows_hbm.at[r, p], rows_hbm.at[r, p], across_send, across_recv,
            device_id=(1 - r, f, t), device_id_type=MESH,
        ).start()
        return carry

    lax.fori_loop(1, FIRST, send_within, 0)
    pltpu.make_async_remote_copy(
        src.at[f], rows_hbm.at[r, f], across_send, across_recv,
        device_id=(1 - r, f, t), device_id_type=MESH,
    ).start()
    own_rows = pltpu.make_async_copy(src.at[f], rows_hbm.at[r, f], local_sem.at[0])
    own_rows.start()

    stack[...] = jnp.zeros_like(stack)
    for copy in loads[4:]:
        copy.wait()
    high, low = split(own_basis(basis, f))
    high2 = high.astype(F32)
    left = jnp.concatenate([(high2 + pltpu.roll(high2, 64, 1)).astype(BF16), low], axis=1)

    def project(l, carry):
        for ref, lanes in ((dout, pl.ds(0, ROWS_OUT)), (ddown, pl.ds(WIDE_OUT, ROWS_DOWN))):
            hi, lo = split(ref[l])
            stack[0:COLS, lanes] = hi
            stack[64 : 64 + COLS, lanes] = lo
            stack[128 : 128 + COLS, lanes] = hi
        coef = jnp.dot(left, stack[...], preferred_element_type=F32)
        for a in range(2):
            for b in range(2):
                rows = coef[PIECE * (2 * a + b) : PIECE * (2 * a + b + 1)]
                part[2 * l + a, b] = rows
                part16[2 * l + a, b] = rows.astype(BF16)
        return carry

    lax.fori_loop(0, 8, project, 0)

    partner_core = (r, 2 * chip + other, t)
    core_copy = pltpu.make_async_remote_copy(
        part16.at[:, other], cross, core_send, core_recv, device_id=partner_core, device_id_type=MESH
    )
    core_copy.start()
    core_copy.wait_recv()

    def halve(p, carry):
        half[p] = (part[p, core] + cross[p].astype(F32)).astype(BF16)
        return carry

    lax.fori_loop(0, CHIPS, halve, 0)
    gathered[chip] = half[chip]

    def send_half(i, carry):
        p = lax.rem(chip + i, CHIPS)
        pltpu.make_async_remote_copy(
            half.at[p], gathered.at[chip], rs_send, rs_recv,
            device_id=(r, 2 * p + core, t), device_id_type=MESH,
        ).start()
        return carry

    lax.fori_loop(1, CHIPS, send_half, 0)
    lax.fori_loop(FIRST, N_FSDP, send_within, 0)
    lax.fori_loop(1, FIRST, send_across, 0)

    rs_wait = pltpu.make_async_remote_copy(
        half.at[pl.ds(0, CHIPS - 1)], gathered.at[pl.ds(0, CHIPS - 1)], rs_send, rs_recv,
        device_id=partner_core, device_id_type=MESH,
    )
    rs_wait.wait_recv()
    total = gathered[0].astype(F32)
    for p in range(1, CHIPS):
        total = total + gathered[p].astype(F32)
    mine[...] = total.astype(BF16)
    rep_copy = pltpu.make_async_remote_copy(
        mine, theirs, rep_send, rep_recv, device_id=(1 - r, f, t), device_id_type=MESH
    )
    rep_copy.start()
    rep_copy.wait_recv()
    final[...] = (0.5 * (mine[...].astype(F32) + theirs[...].astype(F32))).astype(BF16)

    def send_final(i, carry):
        p = lax.rem(chip + i, CHIPS)
        pltpu.make_async_remote_copy(
            final, coef_hbm.at[chip, core], ag_send, ag_recv.at[chip],
            device_id=(r, 2 * p + core, t), device_id_type=MESH,
        ).start()
        return carry

    pltpu.make_async_remote_copy(
        final, coef_hbm.at[chip, core], ag_send, fw_recv, device_id=partner_core, device_id_type=MESH
    ).start()
    lax.fori_loop(1, CHIPS, send_final, 0)
    own_coef = pltpu.make_async_copy(final, coef_hbm.at[chip, core], local_sem.at[1])
    own_coef.start()
    lax.fori_loop(FIRST, N_FSDP, send_across, 0)

    def forward(i, carry):
        p = lax.rem(chip + CHIPS - i, CHIPS)
        pltpu.make_async_remote_copy(
            final, coef_hbm.at[p, core], ag_send, ag_recv.at[p], device_id=partner_core, device_id_type=MESH
        ).wait_recv()
        pltpu.make_async_remote_copy(
            coef_hbm.at[p, core], coef_hbm.at[p, core], fw_send, fw_recv,
            device_id=partner_core, device_id_type=MESH,
        ).start()
        return carry

    lax.fori_loop(1, CHIPS, forward, 0)

    own_rows.wait()
    own_coef.wait()
    core_copy.wait_send()
    rs_wait.wait_send()
    rep_copy.wait_send()

    most = pl.ds(0, N_FSDP - 1)
    pltpu.make_async_remote_copy(
        src.at[most], src.at[most], base_send, across_recv, device_id=partner_core, device_id_type=MESH
    ).wait_send()
    across = pltpu.make_async_remote_copy(
        src, rows_hbm.at[1 - r], across_send, across_recv, device_id=partner_core, device_id_type=MESH
    )
    across.wait_send()
    across.wait_recv()
    pltpu.make_async_remote_copy(
        half, half, ag_send, fw_recv, device_id=partner_core, device_id_type=MESH
    ).wait_send()
    pltpu.make_async_remote_copy(
        half.at[pl.ds(0, CHIPS - 1)], half.at[pl.ds(0, CHIPS - 1)], fw_send, fw_recv,
        device_id=partner_core, device_id_type=MESH,
    ).wait_send()
    pltpu.make_async_remote_copy(
        half, coef_hbm.at[:, other], fw_send, fw_recv, device_id=partner_core, device_id_type=MESH
    ).wait_recv()


def exchange(dout, ddown, basis, aout, adown, mout, mdown):
    any_spec = pl.BlockSpec(memory_space=pl.ANY)
    sem = pltpu.SemaphoreType.DMA
    return pl.pallas_call(
        exchange_kernel,
        name="exchange",
        out_shape=(
            jax.ShapeDtypeStruct((2, N_FSDP, MSG, LANES), BF16),
            jax.ShapeDtypeStruct((CHIPS, 2, PIECE, WIDE), BF16),
        ),
        in_specs=[any_spec] * 7,
        out_specs=(any_spec, any_spec),
        scratch_shapes=[
            pltpu.VMEM(dout.shape, F32),
            pltpu.VMEM(ddown.shape, F32),
            pltpu.VMEM(basis.shape, F32),
            pltpu.VMEM(aout.shape, F32),
            pltpu.VMEM(adown.shape, F32),
            pltpu.VMEM(mout.shape, F32),
            pltpu.VMEM(mdown.shape, F32),
            pltpu.VMEM((256, WIDE), BF16),
            pltpu.VMEM((CHIPS, 2, PIECE, WIDE), F32),
            pltpu.VMEM((CHIPS, 2, PIECE, WIDE), BF16),
            pltpu.VMEM((CHIPS, PIECE, WIDE), BF16),
            pltpu.VMEM((CHIPS, PIECE, WIDE), BF16),
            pltpu.VMEM((CHIPS, PIECE, WIDE), BF16),
            pltpu.VMEM((PIECE, WIDE), BF16),
            pltpu.VMEM((PIECE, WIDE), BF16),
            pltpu.VMEM((PIECE, WIDE), BF16),
            pltpu.VMEM((2, CHUNKS, MSG, LANES), F32),
            pltpu.VMEM((N_FSDP, MSG, LANES), BF16),
            sem((7,)), sem((2,)), sem, sem((N_FSDP,)), sem, sem, sem, sem, sem, sem,
            sem, sem, sem, sem((CHIPS,)), sem, sem,
        ],
        compiler_params=pltpu.CompilerParams(
            collective_id=0, has_side_effects=True, vmem_limit_bytes=56 * 1024 * 1024
        ),
    )(dout, ddown, basis, aout, adown, mout, mdown)


TN = (((0,), (0,)), ((), ()))
NT = (((1,), (1,)), ((), ()))


def placement(first, count, height, shift, own, tile):
    shape = (count, height, 2 * LANES)
    source = lax.broadcasted_iota(jnp.int32, shape, 0) + first
    lane = lax.broadcasted_iota(jnp.int32, shape, 2)
    second = lane >= LANES
    row = jnp.where(second, lane - LANES, lane) + LANES * tile
    at = lax.broadcasted_iota(jnp.int32, shape, 1) - shift - jnp.where(second, own, 0)
    hit = (row - own * source == at) & (at >= 0) & (at < own)
    return jnp.where(hit, 1.0, 0.0).astype(BF16).reshape(count * height, 2 * LANES)


def finish_kernel(
    place, rows, coef, basis, aout, adown, mout, mdown,
    wout, wdown, aout_new, adown_new, mout_new, mdown_new, grad,
):
    r, f = place[0], place[1]
    high, low = split(own_basis(basis, f))
    left = jnp.concatenate([high, low], axis=0)

    def project(l, carry):
        c = coef[l]
        g = lax.dot_general(left, jnp.concatenate([c, c], axis=0), TN, preferred_element_type=F32)
        grad[l] = grad_gain * g[:COLS]
        return carry

    lax.fori_loop(0, 8, project, 0)

    for out, own, count, height, begin, shift, total, lane0 in (
        (wout, OWN_OUT, 10, 32, 0, 0, ROWS_OUT, 0),
        (wdown, OWN_DOWN, 5, 80, 24, 4, ROWS_DOWN, WIDE_OUT),
    ):
        for tile in range((total + LANES - 1) // LANES):
            first = min((LANES * tile) // own, N_FSDP - count)
            pick = placement(first, count, height, shift, own, tile)
            width = min(LANES, total - LANES * tile)
            for g in range(2):
                got = rows[g, first : first + count, begin : begin + height, :].reshape(count * height, LANES)
                placed = lax.dot_general(got, pick, TN, preferred_element_type=F32)
                for h in range(2):
                    for b in range(2):
                        l = 4 * g + 2 * h + b
                        lanes = pl.ds(lane0 + LANES * tile, width)
                        value = placed[64 * h : 64 * h + COLS, LANES * b : LANES * b + width] - grad[l, :, lanes]
                        out[l, :, pl.ds(LANES * tile, width)] = value.astype(BF16)

    bhigh, blow = split(basis[...])
    for a, m, a_new, m_new, own, lane0, wide in (
        (aout, mout, aout_new, mout_new, OWN_OUT, 0, WIDE_OUT),
        (adown, mdown, adown_new, mdown_new, OWN_DOWN, WIDE_OUT, WIDE_DOWN),
    ):
        n = 4 * own
        picked = jnp.zeros((n, 64), F32)
        for l in range(4):
            row = lax.broadcasted_iota(jnp.int32, (n, wide), 0) - own * l
            lane = lax.broadcasted_iota(jnp.int32, (n, wide), 1)
            hit = (lane - own * f == row) & (row >= 0) & (row < own)
            one = jnp.where(hit, 1.0, 0.0).astype(BF16)
            picked = picked + lax.dot_general(
                one, coef[4 * r + l, :, pl.ds(lane0, wide)], NT, preferred_element_type=F32
            )
        picked = picked.astype(BF16)
        step = jnp.dot(picked, bhigh, preferred_element_type=F32) + jnp.dot(
            picked, blow, preferred_element_type=F32
        )
        for c in range(CHUNKS):
            at = pl.ds(c, n, stride=CHUNKS)
            g = step[:, LANES * c : LANES * (c + 1)]
            moment = nesterov_decay * m[at, :] + g
            m_new[at, :] = moment
            a_new[at, :] = a[at, :] - outer_rate * (g + nesterov_decay * moment)


def finish(place, rows, coef, basis, aout, adown, mout, mdown):
    vmem = pl.BlockSpec(memory_space=pltpu.VMEM)
    return pl.pallas_call(
        finish_kernel,
        name="finish",
        out_shape=(
            jax.ShapeDtypeStruct((8, COLS, ROWS_OUT), BF16),
            jax.ShapeDtypeStruct((8, COLS, ROWS_DOWN), BF16),
            jax.ShapeDtypeStruct(aout.shape, F32),
            jax.ShapeDtypeStruct(adown.shape, F32),
            jax.ShapeDtypeStruct(aout.shape, F32),
            jax.ShapeDtypeStruct(adown.shape, F32),
        ),
        in_specs=[pl.BlockSpec(memory_space=pltpu.SMEM)] + [vmem] * 7,
        out_specs=(vmem,) * 6,
        scratch_shapes=[pltpu.VMEM((8, COLS, WIDE), F32)],
        compiler_params=pltpu.CompilerParams(vmem_limit_bytes=56 * 1024 * 1024),
    )(place, rows, coef, basis, aout, adown, mout, mdown)


def per_device(delta_out, delta_down, basis, anchor_out, anchor_down, moment_out, moment_down):
    dout = jnp.transpose(delta_out[0], (0, 2, 1))
    ddown = jnp.transpose(delta_down[0], (0, 2, 1))
    basis_t = basis.T
    flat = [x.reshape(-1, LANES) for x in (anchor_out, anchor_down, moment_out, moment_down)]
    rows, coef = exchange(dout, ddown, basis_t, *flat)
    place = jnp.stack([lax.axis_index("rep"), lax.axis_index("fsdp")]).astype(jnp.int32)
    wout, wdown, aout, adown, mout, mdown = finish(
        place, rows, coef.reshape(8, 64, WIDE), basis_t, *flat
    )
    return (
        jnp.transpose(wout, (0, 2, 1)),
        jnp.transpose(wdown, (0, 2, 1)),
        aout.reshape(anchor_out.shape),
        adown.reshape(anchor_down.shape),
        mout.reshape(moment_out.shape),
        mdown.reshape(moment_down.shape),
    )


def solution(mesh):
    return jax.shard_map(
        per_device,
        mesh=mesh,
        in_specs=(
            P("rep", None, "tp", "fsdp"),
            P("rep", None, "tp", "fsdp"),
            P(),
            P("rep", "tp", "fsdp", None),
            P("rep", "tp", "fsdp", None),
            P("rep", "tp", "fsdp", None),
            P("rep", "tp", "fsdp", None),
        ),
        out_specs=(
            P(None, "tp", "fsdp"),
            P(None, "tp", "fsdp"),
            P("rep", "tp", "fsdp", None),
            P("rep", "tp", "fsdp", None),
            P("rep", "tp", "fsdp", None),
            P("rep", "tp", "fsdp", None),
        ),
        check_vma=False,
    )
```

```python
import jax
import jax.numpy as jnp
from jax import lax
from jax.experimental import pallas as pl
from jax.experimental.pallas import tpu as pltpu
from jax.sharding import PartitionSpec as P

MESH = pl.DeviceIdType.MESH
outer_rate = 0.7
nesterov_decay = 0.9
base_decay = outer_rate * nesterov_decay * nesterov_decay
grad_gain = outer_rate * (1.0 + nesterov_decay)

LANES = 128
COLS = 56
ROWS_OUT, ROWS_DOWN = 448, 1216
OWN_OUT, OWN_DOWN = 14, 38
WIDE_OUT, WIDE_DOWN = 512, 1280
WIDE = WIDE_OUT + WIDE_DOWN
MSG = 2 * (OWN_OUT + OWN_DOWN)
CHUNKS = 14
N_FSDP = 32
CHIPS = 16
PIECE = 16
FIRST = 16
F32, BF16 = jnp.float32, jnp.bfloat16


def column_window(load_chunk, index):
    first = (7 * index) // 16
    offset = COLS * index - LANES * first
    second = jnp.minimum(first + 1, CHUNKS - 1)
    return load_chunk(first), load_chunk(second), offset


def own_basis(basis_ref, f):
    low, high, offset = column_window(
        lambda k: basis_ref[:, pl.ds(pl.multiple_of(k * LANES, LANES), LANES)], f
    )
    lane = lax.broadcasted_iota(jnp.int32, low.shape, 1)
    window = jnp.where(lane >= offset, low, high)
    window = pltpu.roll(window, lax.rem(LANES - offset, LANES), 1)
    return jnp.where(lane < COLS, window, 0.0)


def split(x):
    high = x.astype(BF16)
    return high, (x - high.astype(F32)).astype(BF16)


def exchange_kernel(
    dout_hbm, ddown_hbm, basis_hbm, aout_hbm, adown_hbm, mout_hbm, mdown_hbm,
    rows_hbm, coef_hbm,
    dout, ddown, basis, aout, adown, mout, mdown,
    stack, part, part16, cross, half, gathered, mine, theirs, final, base, src,
    in_sem, local_sem, base_send, base_recv, across_send, across_recv, core_send, core_recv, rs_send, rs_recv,
    rep_send, rep_recv, ag_send, ag_recv, fw_send, fw_recv,
):
    r = lax.axis_index("rep")
    f = lax.axis_index("fsdp")
    t = lax.axis_index("tp")
    chip, core = f // 2, lax.rem(f, 2)
    other = 1 - core

    loads = [
        pltpu.make_async_copy(a, b, in_sem.at[i])
        for i, (a, b) in enumerate(
            ((aout_hbm, aout), (mout_hbm, mout), (adown_hbm, adown), (mdown_hbm, mdown),
             (basis_hbm, basis), (dout_hbm, dout), (ddown_hbm, ddown))
        )
    ]
    for copy in loads:
        copy.start()

    barrier = pltpu.get_barrier_semaphore()

    def greet(i, carry):
        pl.semaphore_signal(
            barrier, inc=1, device_id=(r, lax.rem(f + i, N_FSDP), t), device_id_type=MESH
        )
        return carry

    lax.fori_loop(1, N_FSDP, greet, 0)
    pl.semaphore_signal(barrier, inc=1, device_id=(1 - r, f, t), device_id_type=MESH)

    for copy in loads[:4]:
        copy.wait()

    def combine(c, carry):
        for h in range(2):
            for a, m, count, at in ((aout, mout, 28, 0), (adown, mdown, 76, 28)):
                rows = pl.ds(c + CHUNKS * count * h, count, stride=CHUNKS)
                base[h, c, at : at + count, :] = a[rows, :] - base_decay * m[rows, :]
        return carry

    lax.fori_loop(0, CHUNKS, combine, 0)

    def pack(j, carry):
        low0, high0, offset = column_window(lambda k: base[0, k], j)
        low1, high1, _ = column_window(lambda k: base[1, k], j)
        lane = lax.broadcasted_iota(jnp.int32, low0.shape, 1)
        first = pltpu.roll(jnp.where(lane >= offset, low0, high0), lax.rem(LANES - offset, LANES), 1)
        second = pltpu.roll(jnp.where(lane >= offset, low1, high1), lax.rem(LANES + 64 - offset, LANES), 1)
        src[j] = jnp.where(lane < 64, first, second).astype(BF16)
        return carry

    lax.fori_loop(0, N_FSDP, pack, 0)

    pl.semaphore_wait(barrier, N_FSDP)

    def send_within(i, carry):
        j = lax.rem(f + i, N_FSDP)
        pltpu.make_async_remote_copy(
            src.at[j], rows_hbm.at[r, f], base_send, base_recv.at[f],
            device_id=(r, j, t), device_id_type=MESH,
        ).start()
        return carry

    def send_across(i, carry):
        p = lax.rem(f + N_FSDP - i, N_FSDP)
        pltpu.make_async_remote_copy(
            src.at[p], rows_hbm.at[r, p], base_send, base_recv.at[p],
            device_id=(1 - r, f, t), device_id_type=MESH,
        ).wait_recv()
        pltpu.make_async_remote_copy(
            rows_hbm.at[r, p], rows_hbm.at[r, p], across_send, across_recv,
            device_id=(1 - r, f, t), device_id_type=MESH,
        ).start()
        return carry

    lax.fori_loop(1, FIRST, send_within, 0)
    pltpu.make_async_remote_copy(
        src.at[f], rows_hbm.at[r, f], across_send, across_recv,
        device_id=(1 - r, f, t), device_id_type=MESH,
    ).start()
    own_rows = pltpu.make_async_copy(src.at[f], rows_hbm.at[r, f], local_sem.at[0])
    own_rows.start()

    stack[...] = jnp.zeros_like(stack)
    for copy in loads[4:]:
        copy.wait()
    high, low = split(own_basis(basis, f))
    high2 = high.astype(F32)
    left = jnp.concatenate([(high2 + pltpu.roll(high2, 64, 1)).astype(BF16), low], axis=1)

    def project(l, carry):
        for ref, lanes in ((dout, pl.ds(0, ROWS_OUT)), (ddown, pl.ds(WIDE_OUT, ROWS_DOWN))):
            hi, lo = split(ref[l])
            stack[0:COLS, lanes] = hi
            stack[64 : 64 + COLS, lanes] = lo
            stack[128 : 128 + COLS, lanes] = hi
        coef = jnp.dot(left, stack[...], preferred_element_type=F32)
        for a in range(2):
            for b in range(2):
                rows = coef[PIECE * (2 * a + b) : PIECE * (2 * a + b + 1)]
                part[2 * l + a, b] = rows
                part16[2 * l + a, b] = rows.astype(BF16)
        return carry

    lax.fori_loop(0, 8, project, 0)

    partner_core = (r, 2 * chip + other, t)
    core_copy = pltpu.make_async_remote_copy(
        part16.at[:, other], cross, core_send, core_recv, device_id=partner_core, device_id_type=MESH
    )
    core_copy.start()
    core_copy.wait_recv()

    def halve(p, carry):
        half[p] = (part[p, core] + cross[p].astype(F32)).astype(BF16)
        return carry

    lax.fori_loop(0, CHIPS, halve, 0)
    gathered[chip] = half[chip]

    def send_half(i, carry):
        p = lax.rem(chip + i, CHIPS)
        pltpu.make_async_remote_copy(
            half.at[p], gathered.at[chip], rs_send, rs_recv,
            device_id=(r, 2 * p + core, t), device_id_type=MESH,
        ).start()
        return carry

    lax.fori_loop(1, CHIPS, send_half, 0)
    lax.fori_loop(FIRST, N_FSDP, send_within, 0)
    lax.fori_loop(1, FIRST, send_across, 0)

    rs_wait = pltpu.make_async_remote_copy(
        half.at[pl.ds(0, CHIPS - 1)], gathered.at[pl.ds(0, CHIPS - 1)], rs_send, rs_recv,
        device_id=partner_core, device_id_type=MESH,
    )
    rs_wait.wait_recv()
    total = gathered[0].astype(F32)
    for p in range(1, CHIPS):
        total = total + gathered[p].astype(F32)
    mine[...] = total.astype(BF16)
    rep_copy = pltpu.make_async_remote_copy(
        mine, theirs, rep_send, rep_recv, device_id=(1 - r, f, t), device_id_type=MESH
    )
    rep_copy.start()
    rep_copy.wait_recv()
    final[...] = (0.5 * (mine[...].astype(F32) + theirs[...].astype(F32))).astype(BF16)

    x, y = lax.rem(chip, 4), chip // 4
    stride_u, stride_v = 1 + 3 * core, 4 - 3 * core
    u = (1 - core) * x + core * y
    v = (1 - core) * y + core * x

    def chip_at(du, dv):
        return lax.rem(u + du, 4) * stride_u + lax.rem(v + dv, 4) * stride_v

    def send_coef(source, s, target):
        pltpu.make_async_remote_copy(
            source, coef_hbm.at[s, core], ag_send, ag_recv.at[s],
            device_id=(r, 2 * target + core, t), device_id_type=MESH,
        ).start()

    def send_final_u(i, carry):
        send_coef(final, chip, chip_at(i, 0))
        return carry

    def send_final_v(i, carry):
        send_coef(final, chip, chip_at(0, i))
        return carry

    def forward(s):
        pltpu.make_async_remote_copy(
            final, coef_hbm.at[s, core], ag_send, ag_recv.at[s], device_id=partner_core, device_id_type=MESH
        ).wait_recv()
        pltpu.make_async_remote_copy(
            coef_hbm.at[s, core], coef_hbm.at[s, core], fw_send, fw_recv,
            device_id=partner_core, device_id_type=MESH,
        ).start()

    def relay(k, carry):
        s = chip_at(4 - k, 0)
        forward(s)

        def send(i, inner):
            send_coef(coef_hbm.at[s, core], s, chip_at(0, i))
            return inner

        return lax.fori_loop(1, 4, send, carry)

    def collect(i, carry):
        forward(chip_at(i // 3, 1 + lax.rem(i, 3)))
        return carry

    lax.fori_loop(1, 4, send_final_u, 0)
    pltpu.make_async_remote_copy(
        final, coef_hbm.at[chip, core], ag_send, fw_recv, device_id=partner_core, device_id_type=MESH
    ).start()
    lax.fori_loop(1, 4, send_final_v, 0)
    own_coef = pltpu.make_async_copy(final, coef_hbm.at[chip, core], local_sem.at[1])
    own_coef.start()
    lax.fori_loop(FIRST, 24, send_across, 0)
    lax.fori_loop(1, 4, relay, 0)
    lax.fori_loop(24, N_FSDP, send_across, 0)
    lax.fori_loop(0, 12, collect, 0)

    own_rows.wait()
    own_coef.wait()
    core_copy.wait_send()
    rs_wait.wait_send()
    rep_copy.wait_send()

    most = pl.ds(0, N_FSDP - 1)
    pltpu.make_async_remote_copy(
        src.at[most], src.at[most], base_send, across_recv, device_id=partner_core, device_id_type=MESH
    ).wait_send()
    across = pltpu.make_async_remote_copy(
        src, rows_hbm.at[1 - r], across_send, across_recv, device_id=partner_core, device_id_type=MESH
    )
    across.wait_send()
    across.wait_recv()
    pltpu.make_async_remote_copy(
        half, half, ag_send, fw_recv, device_id=partner_core, device_id_type=MESH
    ).wait_send()
    pltpu.make_async_remote_copy(
        half.at[pl.ds(0, CHIPS - 1)], half.at[pl.ds(0, CHIPS - 1)], fw_send, fw_recv,
        device_id=partner_core, device_id_type=MESH,
    ).wait_send()
    pltpu.make_async_remote_copy(
        half, coef_hbm.at[:, other], fw_send, fw_recv, device_id=partner_core, device_id_type=MESH
    ).wait_recv()


def exchange(dout, ddown, basis, aout, adown, mout, mdown):
    any_spec = pl.BlockSpec(memory_space=pl.ANY)
    sem = pltpu.SemaphoreType.DMA
    return pl.pallas_call(
        exchange_kernel,
        name="exchange",
        out_shape=(
            jax.ShapeDtypeStruct((2, N_FSDP, MSG, LANES), BF16),
            jax.ShapeDtypeStruct((CHIPS, 2, PIECE, WIDE), BF16),
        ),
        in_specs=[any_spec] * 7,
        out_specs=(any_spec, any_spec),
        scratch_shapes=[
            pltpu.VMEM(dout.shape, F32),
            pltpu.VMEM(ddown.shape, F32),
            pltpu.VMEM(basis.shape, F32),
            pltpu.VMEM(aout.shape, F32),
            pltpu.VMEM(adown.shape, F32),
            pltpu.VMEM(mout.shape, F32),
            pltpu.VMEM(mdown.shape, F32),
            pltpu.VMEM((256, WIDE), BF16),
            pltpu.VMEM((CHIPS, 2, PIECE, WIDE), F32),
            pltpu.VMEM((CHIPS, 2, PIECE, WIDE), BF16),
            pltpu.VMEM((CHIPS, PIECE, WIDE), BF16),
            pltpu.VMEM((CHIPS, PIECE, WIDE), BF16),
            pltpu.VMEM((CHIPS, PIECE, WIDE), BF16),
            pltpu.VMEM((PIECE, WIDE), BF16),
            pltpu.VMEM((PIECE, WIDE), BF16),
            pltpu.VMEM((PIECE, WIDE), BF16),
            pltpu.VMEM((2, CHUNKS, MSG, LANES), F32),
            pltpu.VMEM((N_FSDP, MSG, LANES), BF16),
            sem((7,)), sem((2,)), sem, sem((N_FSDP,)), sem, sem, sem, sem, sem, sem,
            sem, sem, sem, sem((CHIPS,)), sem, sem,
        ],
        compiler_params=pltpu.CompilerParams(
            collective_id=0, has_side_effects=True, vmem_limit_bytes=56 * 1024 * 1024
        ),
    )(dout, ddown, basis, aout, adown, mout, mdown)


TN = (((0,), (0,)), ((), ()))
NT = (((1,), (1,)), ((), ()))


def placement(first, count, height, shift, own, tile):
    shape = (count, height, 2 * LANES)
    source = lax.broadcasted_iota(jnp.int32, shape, 0) + first
    lane = lax.broadcasted_iota(jnp.int32, shape, 2)
    second = lane >= LANES
    row = jnp.where(second, lane - LANES, lane) + LANES * tile
    at = lax.broadcasted_iota(jnp.int32, shape, 1) - shift - jnp.where(second, own, 0)
    hit = (row - own * source == at) & (at >= 0) & (at < own)
    return jnp.where(hit, 1.0, 0.0).astype(BF16).reshape(count * height, 2 * LANES)


def finish_kernel(
    place, rows, coef, basis, aout, adown, mout, mdown,
    wout, wdown, aout_new, adown_new, mout_new, mdown_new, grad,
):
    r, f = place[0], place[1]
    high, low = split(own_basis(basis, f))
    left = jnp.concatenate([high, low], axis=0)

    def project(l, carry):
        c = coef[l]
        g = lax.dot_general(left, jnp.concatenate([c, c], axis=0), TN, preferred_element_type=F32)
        grad[l] = grad_gain * g[:COLS]
        return carry

    lax.fori_loop(0, 8, project, 0)

    for out, own, count, height, begin, shift, total, lane0 in (
        (wout, OWN_OUT, 10, 32, 0, 0, ROWS_OUT, 0),
        (wdown, OWN_DOWN, 5, 80, 24, 4, ROWS_DOWN, WIDE_OUT),
    ):
        for tile in range((total + LANES - 1) // LANES):
            first = min((LANES * tile) // own, N_FSDP - count)
            pick = placement(first, count, height, shift, own, tile)
            width = min(LANES, total - LANES * tile)
            for g in range(2):
                got = rows[g, first : first + count, begin : begin + height, :].reshape(count * height, LANES)
                placed = lax.dot_general(got, pick, TN, preferred_element_type=F32)
                for h in range(2):
                    for b in range(2):
                        l = 4 * g + 2 * h + b
                        lanes = pl.ds(lane0 + LANES * tile, width)
                        value = placed[64 * h : 64 * h + COLS, LANES * b : LANES * b + width] - grad[l, :, lanes]
                        out[l, :, pl.ds(LANES * tile, width)] = value.astype(BF16)

    bhigh, blow = split(basis[...])
    for a, m, a_new, m_new, own, lane0, wide in (
        (aout, mout, aout_new, mout_new, OWN_OUT, 0, WIDE_OUT),
        (adown, mdown, adown_new, mdown_new, OWN_DOWN, WIDE_OUT, WIDE_DOWN),
    ):
        n = 4 * own
        picked = jnp.zeros((n, 64), F32)
        for l in range(4):
            row = lax.broadcasted_iota(jnp.int32, (n, wide), 0) - own * l
            lane = lax.broadcasted_iota(jnp.int32, (n, wide), 1)
            hit = (lane - own * f == row) & (row >= 0) & (row < own)
            one = jnp.where(hit, 1.0, 0.0).astype(BF16)
            picked = picked + lax.dot_general(
                one, coef[4 * r + l, :, pl.ds(lane0, wide)], NT, preferred_element_type=F32
            )
        picked = picked.astype(BF16)
        step = jnp.dot(picked, bhigh, preferred_element_type=F32) + jnp.dot(
            picked, blow, preferred_element_type=F32
        )
        for c in range(CHUNKS):
            at = pl.ds(c, n, stride=CHUNKS)
            g = step[:, LANES * c : LANES * (c + 1)]
            moment = nesterov_decay * m[at, :] + g
            m_new[at, :] = moment
            a_new[at, :] = a[at, :] - outer_rate * (g + nesterov_decay * moment)


def finish(place, rows, coef, basis, aout, adown, mout, mdown):
    vmem = pl.BlockSpec(memory_space=pltpu.VMEM)
    return pl.pallas_call(
        finish_kernel,
        name="finish",
        out_shape=(
            jax.ShapeDtypeStruct((8, COLS, ROWS_OUT), BF16),
            jax.ShapeDtypeStruct((8, COLS, ROWS_DOWN), BF16),
            jax.ShapeDtypeStruct(aout.shape, F32),
            jax.ShapeDtypeStruct(adown.shape, F32),
            jax.ShapeDtypeStruct(aout.shape, F32),
            jax.ShapeDtypeStruct(adown.shape, F32),
        ),
        in_specs=[pl.BlockSpec(memory_space=pltpu.SMEM)] + [vmem] * 7,
        out_specs=(vmem,) * 6,
        scratch_shapes=[pltpu.VMEM((8, COLS, WIDE), F32)],
        compiler_params=pltpu.CompilerParams(vmem_limit_bytes=56 * 1024 * 1024),
    )(place, rows, coef, basis, aout, adown, mout, mdown)


def per_device(delta_out, delta_down, basis, anchor_out, anchor_down, moment_out, moment_down):
    dout = jnp.transpose(delta_out[0], (0, 2, 1))
    ddown = jnp.transpose(delta_down[0], (0, 2, 1))
    basis_t = basis.T
    flat = [x.reshape(-1, LANES) for x in (anchor_out, anchor_down, moment_out, moment_down)]
    rows, coef = exchange(dout, ddown, basis_t, *flat)
    place = jnp.stack([lax.axis_index("rep"), lax.axis_index("fsdp")]).astype(jnp.int32)
    wout, wdown, aout, adown, mout, mdown = finish(
        place, rows, coef.reshape(8, 64, WIDE), basis_t, *flat
    )
    return (
        jnp.transpose(wout, (0, 2, 1)),
        jnp.transpose(wdown, (0, 2, 1)),
        aout.reshape(anchor_out.shape),
        adown.reshape(anchor_down.shape),
        mout.reshape(moment_out.shape),
        mdown.reshape(moment_down.shape),
    )


def solution(mesh):
    return jax.shard_map(
        per_device,
        mesh=mesh,
        in_specs=(
            P("rep", None, "tp", "fsdp"),
            P("rep", None, "tp", "fsdp"),
            P(),
            P("rep", "tp", "fsdp", None),
            P("rep", "tp", "fsdp", None),
            P("rep", "tp", "fsdp", None),
            P("rep", "tp", "fsdp", None),
        ),
        out_specs=(
            P(None, "tp", "fsdp"),
            P(None, "tp", "fsdp"),
            P("rep", "tp", "fsdp", None),
            P("rep", "tp", "fsdp", None),
            P("rep", "tp", "fsdp", None),
            P("rep", "tp", "fsdp", None),
        ),
        check_vma=False,
    )
```

```python
import jax
import jax.numpy as jnp
from jax import lax
from jax.experimental import pallas as pl
from jax.experimental.pallas import tpu as pltpu
from jax.sharding import PartitionSpec as P

MESH = pl.DeviceIdType.MESH
outer_rate = 0.7
nesterov_decay = 0.9
base_decay = outer_rate * nesterov_decay * nesterov_decay
grad_gain = outer_rate * (1.0 + nesterov_decay)

LANES = 128
COLS = 56
ROWS_OUT, ROWS_DOWN = 448, 1216
OWN_OUT, OWN_DOWN = 14, 38
WIDE_OUT, WIDE_DOWN = 512, 1280
WIDE = WIDE_OUT + WIDE_DOWN
MSG = 2 * (OWN_OUT + OWN_DOWN)
CHUNKS = 14
N_FSDP = 32
CHIPS = 16
PIECE = 16
FIRST = 16
F32, BF16 = jnp.float32, jnp.bfloat16


def column_window(load_chunk, index):
    first = (7 * index) // 16
    offset = COLS * index - LANES * first
    second = jnp.minimum(first + 1, CHUNKS - 1)
    return load_chunk(first), load_chunk(second), offset


def own_basis(basis_ref, f):
    low, high, offset = column_window(
        lambda k: basis_ref[:, pl.ds(pl.multiple_of(k * LANES, LANES), LANES)], f
    )
    lane = lax.broadcasted_iota(jnp.int32, low.shape, 1)
    window = jnp.where(lane >= offset, low, high)
    window = pltpu.roll(window, lax.rem(LANES - offset, LANES), 1)
    return jnp.where(lane < COLS, window, 0.0)


def split(x):
    high = x.astype(BF16)
    return high, (x - high.astype(F32)).astype(BF16)


def exchange_kernel(
    dout_hbm, ddown_hbm, basis_hbm, aout_hbm, adown_hbm, mout_hbm, mdown_hbm,
    rows_hbm, coef_hbm,
    dout, ddown, basis, aout, adown, mout, mdown,
    stack, part, part16, cross, half, gathered, line, landed, mine, theirs, final, base, src,
    in_sem, local_sem, base_send, base_recv, across_send, across_recv, core_send, core_recv, rs_send, rs_recv,
    rep_send, rep_recv, ag_send, ag_recv, fw_send, fw_recv, line_send, line_recv,
):
    r = lax.axis_index("rep")
    f = lax.axis_index("fsdp")
    t = lax.axis_index("tp")
    chip, core = f // 2, lax.rem(f, 2)
    other = 1 - core

    loads = [
        pltpu.make_async_copy(a, b, in_sem.at[i])
        for i, (a, b) in enumerate(
            ((aout_hbm, aout), (mout_hbm, mout), (adown_hbm, adown), (mdown_hbm, mdown),
             (basis_hbm, basis), (dout_hbm, dout), (ddown_hbm, ddown))
        )
    ]
    for copy in loads:
        copy.start()

    barrier = pltpu.get_barrier_semaphore()

    def greet(i, carry):
        pl.semaphore_signal(
            barrier, inc=1, device_id=(r, lax.rem(f + i, N_FSDP), t), device_id_type=MESH
        )
        return carry

    lax.fori_loop(1, N_FSDP, greet, 0)
    pl.semaphore_signal(barrier, inc=1, device_id=(1 - r, f, t), device_id_type=MESH)

    for copy in loads[:4]:
        copy.wait()

    def combine(c, carry):
        for h in range(2):
            for a, m, count, at in ((aout, mout, 28, 0), (adown, mdown, 76, 28)):
                rows = pl.ds(c + CHUNKS * count * h, count, stride=CHUNKS)
                base[h, c, at : at + count, :] = a[rows, :] - base_decay * m[rows, :]
        return carry

    lax.fori_loop(0, CHUNKS, combine, 0)

    def pack(j, carry):
        low0, high0, offset = column_window(lambda k: base[0, k], j)
        low1, high1, _ = column_window(lambda k: base[1, k], j)
        lane = lax.broadcasted_iota(jnp.int32, low0.shape, 1)
        first = pltpu.roll(jnp.where(lane >= offset, low0, high0), lax.rem(LANES - offset, LANES), 1)
        second = pltpu.roll(jnp.where(lane >= offset, low1, high1), lax.rem(LANES + 64 - offset, LANES), 1)
        src[j] = jnp.where(lane < 64, first, second).astype(BF16)
        return carry

    lax.fori_loop(0, N_FSDP, pack, 0)

    pl.semaphore_wait(barrier, N_FSDP)

    def send_within(i, carry):
        j = lax.rem(f + i, N_FSDP)
        pltpu.make_async_remote_copy(
            src.at[j], rows_hbm.at[r, f], base_send, base_recv.at[f],
            device_id=(r, j, t), device_id_type=MESH,
        ).start()
        return carry

    def send_across(i, carry):
        p = lax.rem(f + N_FSDP - i, N_FSDP)
        pltpu.make_async_remote_copy(
            src.at[p], rows_hbm.at[r, p], base_send, base_recv.at[p],
            device_id=(1 - r, f, t), device_id_type=MESH,
        ).wait_recv()
        pltpu.make_async_remote_copy(
            rows_hbm.at[r, p], rows_hbm.at[r, p], across_send, across_recv,
            device_id=(1 - r, f, t), device_id_type=MESH,
        ).start()
        return carry

    lax.fori_loop(1, FIRST, send_within, 0)
    pltpu.make_async_remote_copy(
        src.at[f], rows_hbm.at[r, f], across_send, across_recv,
        device_id=(1 - r, f, t), device_id_type=MESH,
    ).start()
    own_rows = pltpu.make_async_copy(src.at[f], rows_hbm.at[r, f], local_sem.at[0])
    own_rows.start()

    stack[...] = jnp.zeros_like(stack)
    for copy in loads[4:]:
        copy.wait()
    high, low = split(own_basis(basis, f))
    high2 = high.astype(F32)
    left = jnp.concatenate([(high2 + pltpu.roll(high2, 64, 1)).astype(BF16), low], axis=1)

    def project(l, carry):
        for ref, lanes in ((dout, pl.ds(0, ROWS_OUT)), (ddown, pl.ds(WIDE_OUT, ROWS_DOWN))):
            hi, lo = split(ref[l])
            stack[0:COLS, lanes] = hi
            stack[64 : 64 + COLS, lanes] = lo
            stack[128 : 128 + COLS, lanes] = hi
        coef = jnp.dot(left, stack[...], preferred_element_type=F32)
        for a in range(2):
            for b in range(2):
                rows = coef[PIECE * (2 * a + b) : PIECE * (2 * a + b + 1)]
                part[2 * l + a, b] = rows
                part16[2 * l + a, b] = rows.astype(BF16)
        return carry

    lax.fori_loop(0, 8, project, 0)

    partner_core = (r, 2 * chip + other, t)
    core_copy = pltpu.make_async_remote_copy(
        part16.at[:, other], cross, core_send, core_recv, device_id=partner_core, device_id_type=MESH
    )
    core_copy.start()
    core_copy.wait_recv()

    def halve(p, carry):
        half[p] = (part[p, core] + cross[p].astype(F32)).astype(BF16)
        return carry

    lax.fori_loop(0, CHIPS, halve, 0)
    x, y = lax.rem(chip, 4), chip // 4
    stride_u, stride_v = 1 + 3 * core, 4 - 3 * core
    u = (1 - core) * x + core * y
    v = (1 - core) * y + core * x

    def chip_at(du, dv):
        return lax.rem(u + du, 4) * stride_u + lax.rem(v + dv, 4) * stride_v

    for w in range(4):
        gathered[4 * u + w] = half[u * stride_u + w * stride_v]

    def send_half(i, carry):
        du, w = 1 + i // 4, lax.rem(i, 4)
        pltpu.make_async_remote_copy(
            half.at[lax.rem(u + du, 4) * stride_u + w * stride_v], gathered.at[4 * u + w], rs_send, rs_recv,
            device_id=(r, 2 * chip_at(du, 0) + core, t), device_id_type=MESH,
        ).start()
        return carry

    lax.fori_loop(0, 12, send_half, 0)
    lax.fori_loop(1, FIRST, send_across, 0)

    rs_wait = pltpu.make_async_remote_copy(
        half.at[pl.ds(0, 12)], gathered.at[pl.ds(0, 12)], rs_send, rs_recv,
        device_id=partner_core, device_id_type=MESH,
    )
    rs_wait.wait_recv()
    for w in range(4):
        total = gathered[w].astype(F32)
        for p in range(1, 4):
            total = total + gathered[4 * p + w].astype(F32)
        line[w] = total.astype(BF16)
    landed[v] = line[v]

    def send_line(i, carry):
        pltpu.make_async_remote_copy(
            line.at[lax.rem(v + i, 4)], landed.at[v], line_send, line_recv,
            device_id=(r, 2 * chip_at(0, i) + core, t), device_id_type=MESH,
        ).start()
        return carry

    lax.fori_loop(1, 4, send_line, 0)
    lax.fori_loop(FIRST, N_FSDP, send_within, 0)
    line_wait = pltpu.make_async_remote_copy(
        line.at[pl.ds(0, 3)], landed.at[pl.ds(0, 3)], line_send, line_recv,
        device_id=partner_core, device_id_type=MESH,
    )
    line_wait.wait_recv()
    total = landed[0].astype(F32)
    for p in range(1, 4):
        total = total + landed[p].astype(F32)
    mine[...] = total.astype(BF16)
    rep_copy = pltpu.make_async_remote_copy(
        mine, theirs, rep_send, rep_recv, device_id=(1 - r, f, t), device_id_type=MESH
    )
    rep_copy.start()
    rep_copy.wait_recv()
    final[...] = (0.5 * (mine[...].astype(F32) + theirs[...].astype(F32))).astype(BF16)

    def send_coef(source, s, target):
        pltpu.make_async_remote_copy(
            source, coef_hbm.at[s, core], ag_send, ag_recv.at[s],
            device_id=(r, 2 * target + core, t), device_id_type=MESH,
        ).start()

    def send_final_u(i, carry):
        send_coef(final, chip, chip_at(i, 0))
        return carry

    def send_final_v(i, carry):
        send_coef(final, chip, chip_at(0, i))
        return carry

    def forward(s):
        pltpu.make_async_remote_copy(
            final, coef_hbm.at[s, core], ag_send, ag_recv.at[s], device_id=partner_core, device_id_type=MESH
        ).wait_recv()
        pltpu.make_async_remote_copy(
            coef_hbm.at[s, core], coef_hbm.at[s, core], fw_send, fw_recv,
            device_id=partner_core, device_id_type=MESH,
        ).start()

    def relay(k, carry):
        s = chip_at(4 - k, 0)
        forward(s)

        def send(i, inner):
            send_coef(coef_hbm.at[s, core], s, chip_at(0, i))
            return inner

        return lax.fori_loop(1, 4, send, carry)

    def collect(i, carry):
        forward(chip_at(i // 3, 1 + lax.rem(i, 3)))
        return carry

    lax.fori_loop(1, 4, send_final_u, 0)
    pltpu.make_async_remote_copy(
        final, coef_hbm.at[chip, core], ag_send, fw_recv, device_id=partner_core, device_id_type=MESH
    ).start()
    lax.fori_loop(1, 4, send_final_v, 0)
    own_coef = pltpu.make_async_copy(final, coef_hbm.at[chip, core], local_sem.at[1])
    own_coef.start()
    lax.fori_loop(FIRST, 24, send_across, 0)
    lax.fori_loop(1, 4, relay, 0)
    lax.fori_loop(24, N_FSDP, send_across, 0)
    lax.fori_loop(0, 12, collect, 0)

    own_rows.wait()
    own_coef.wait()
    core_copy.wait_send()
    rs_wait.wait_send()
    line_wait.wait_send()
    rep_copy.wait_send()

    most = pl.ds(0, N_FSDP - 1)
    pltpu.make_async_remote_copy(
        src.at[most], src.at[most], base_send, across_recv, device_id=partner_core, device_id_type=MESH
    ).wait_send()
    across = pltpu.make_async_remote_copy(
        src, rows_hbm.at[1 - r], across_send, across_recv, device_id=partner_core, device_id_type=MESH
    )
    across.wait_send()
    across.wait_recv()
    pltpu.make_async_remote_copy(
        half, half, ag_send, fw_recv, device_id=partner_core, device_id_type=MESH
    ).wait_send()
    pltpu.make_async_remote_copy(
        half.at[pl.ds(0, CHIPS - 1)], half.at[pl.ds(0, CHIPS - 1)], fw_send, fw_recv,
        device_id=partner_core, device_id_type=MESH,
    ).wait_send()
    pltpu.make_async_remote_copy(
        half, coef_hbm.at[:, other], fw_send, fw_recv, device_id=partner_core, device_id_type=MESH
    ).wait_recv()


def exchange(dout, ddown, basis, aout, adown, mout, mdown):
    any_spec = pl.BlockSpec(memory_space=pl.ANY)
    sem = pltpu.SemaphoreType.DMA
    return pl.pallas_call(
        exchange_kernel,
        name="exchange",
        out_shape=(
            jax.ShapeDtypeStruct((2, N_FSDP, MSG, LANES), BF16),
            jax.ShapeDtypeStruct((CHIPS, 2, PIECE, WIDE), BF16),
        ),
        in_specs=[any_spec] * 7,
        out_specs=(any_spec, any_spec),
        scratch_shapes=[
            pltpu.VMEM(dout.shape, F32),
            pltpu.VMEM(ddown.shape, F32),
            pltpu.VMEM(basis.shape, F32),
            pltpu.VMEM(aout.shape, F32),
            pltpu.VMEM(adown.shape, F32),
            pltpu.VMEM(mout.shape, F32),
            pltpu.VMEM(mdown.shape, F32),
            pltpu.VMEM((256, WIDE), BF16),
            pltpu.VMEM((CHIPS, 2, PIECE, WIDE), F32),
            pltpu.VMEM((CHIPS, 2, PIECE, WIDE), BF16),
            pltpu.VMEM((CHIPS, PIECE, WIDE), BF16),
            pltpu.VMEM((CHIPS, PIECE, WIDE), BF16),
            pltpu.VMEM((CHIPS, PIECE, WIDE), BF16),
            pltpu.VMEM((4, PIECE, WIDE), BF16),
            pltpu.VMEM((4, PIECE, WIDE), BF16),
            pltpu.VMEM((PIECE, WIDE), BF16),
            pltpu.VMEM((PIECE, WIDE), BF16),
            pltpu.VMEM((PIECE, WIDE), BF16),
            pltpu.VMEM((2, CHUNKS, MSG, LANES), F32),
            pltpu.VMEM((N_FSDP, MSG, LANES), BF16),
            sem((7,)), sem((2,)), sem, sem((N_FSDP,)), sem, sem, sem, sem, sem, sem,
            sem, sem, sem, sem((CHIPS,)), sem, sem, sem, sem,
        ],
        compiler_params=pltpu.CompilerParams(
            collective_id=0, has_side_effects=True, vmem_limit_bytes=56 * 1024 * 1024
        ),
    )(dout, ddown, basis, aout, adown, mout, mdown)


TN = (((0,), (0,)), ((), ()))
NT = (((1,), (1,)), ((), ()))


def placement(first, count, height, shift, own, tile):
    shape = (count, height, 2 * LANES)
    source = lax.broadcasted_iota(jnp.int32, shape, 0) + first
    lane = lax.broadcasted_iota(jnp.int32, shape, 2)
    second = lane >= LANES
    row = jnp.where(second, lane - LANES, lane) + LANES * tile
    at = lax.broadcasted_iota(jnp.int32, shape, 1) - shift - jnp.where(second, own, 0)
    hit = (row - own * source == at) & (at >= 0) & (at < own)
    return jnp.where(hit, 1.0, 0.0).astype(BF16).reshape(count * height, 2 * LANES)


def finish_kernel(
    place, rows, coef, basis, aout, adown, mout, mdown,
    wout, wdown, aout_new, adown_new, mout_new, mdown_new, grad,
):
    r, f = place[0], place[1]
    high, low = split(own_basis(basis, f))
    left = jnp.concatenate([high, low], axis=0)

    def project(l, carry):
        c = coef[l]
        g = lax.dot_general(left, jnp.concatenate([c, c], axis=0), TN, preferred_element_type=F32)
        grad[l] = grad_gain * g[:COLS]
        return carry

    lax.fori_loop(0, 8, project, 0)

    for out, own, count, height, begin, shift, total, lane0 in (
        (wout, OWN_OUT, 10, 32, 0, 0, ROWS_OUT, 0),
        (wdown, OWN_DOWN, 5, 80, 24, 4, ROWS_DOWN, WIDE_OUT),
    ):
        for tile in range((total + LANES - 1) // LANES):
            first = min((LANES * tile) // own, N_FSDP - count)
            pick = placement(first, count, height, shift, own, tile)
            width = min(LANES, total - LANES * tile)
            for g in range(2):
                got = rows[g, first : first + count, begin : begin + height, :].reshape(count * height, LANES)
                placed = lax.dot_general(got, pick, TN, preferred_element_type=F32)
                for h in range(2):
                    for b in range(2):
                        l = 4 * g + 2 * h + b
                        lanes = pl.ds(lane0 + LANES * tile, width)
                        value = placed[64 * h : 64 * h + COLS, LANES * b : LANES * b + width] - grad[l, :, lanes]
                        out[l, :, pl.ds(LANES * tile, width)] = value.astype(BF16)

    bhigh, blow = split(basis[...])
    for a, m, a_new, m_new, own, lane0, wide in (
        (aout, mout, aout_new, mout_new, OWN_OUT, 0, WIDE_OUT),
        (adown, mdown, adown_new, mdown_new, OWN_DOWN, WIDE_OUT, WIDE_DOWN),
    ):
        n = 4 * own
        picked = jnp.zeros((n, 64), F32)
        for l in range(4):
            row = lax.broadcasted_iota(jnp.int32, (n, wide), 0) - own * l
            lane = lax.broadcasted_iota(jnp.int32, (n, wide), 1)
            hit = (lane - own * f == row) & (row >= 0) & (row < own)
            one = jnp.where(hit, 1.0, 0.0).astype(BF16)
            picked = picked + lax.dot_general(
                one, coef[4 * r + l, :, pl.ds(lane0, wide)], NT, preferred_element_type=F32
            )
        picked = picked.astype(BF16)
        step = jnp.dot(picked, bhigh, preferred_element_type=F32) + jnp.dot(
            picked, blow, preferred_element_type=F32
        )
        for c in range(CHUNKS):
            at = pl.ds(c, n, stride=CHUNKS)
            g = step[:, LANES * c : LANES * (c + 1)]
            moment = nesterov_decay * m[at, :] + g
            m_new[at, :] = moment
            a_new[at, :] = a[at, :] - outer_rate * (g + nesterov_decay * moment)


def finish(place, rows, coef, basis, aout, adown, mout, mdown):
    vmem = pl.BlockSpec(memory_space=pltpu.VMEM)
    return pl.pallas_call(
        finish_kernel,
        name="finish",
        out_shape=(
            jax.ShapeDtypeStruct((8, COLS, ROWS_OUT), BF16),
            jax.ShapeDtypeStruct((8, COLS, ROWS_DOWN), BF16),
            jax.ShapeDtypeStruct(aout.shape, F32),
            jax.ShapeDtypeStruct(adown.shape, F32),
            jax.ShapeDtypeStruct(aout.shape, F32),
            jax.ShapeDtypeStruct(adown.shape, F32),
        ),
        in_specs=[pl.BlockSpec(memory_space=pltpu.SMEM)] + [vmem] * 7,
        out_specs=(vmem,) * 6,
        scratch_shapes=[pltpu.VMEM((8, COLS, WIDE), F32)],
        compiler_params=pltpu.CompilerParams(vmem_limit_bytes=56 * 1024 * 1024),
    )(place, rows, coef, basis, aout, adown, mout, mdown)


def per_device(delta_out, delta_down, basis, anchor_out, anchor_down, moment_out, moment_down):
    dout = jnp.transpose(delta_out[0], (0, 2, 1))
    ddown = jnp.transpose(delta_down[0], (0, 2, 1))
    basis_t = basis.T
    flat = [x.reshape(-1, LANES) for x in (anchor_out, anchor_down, moment_out, moment_down)]
    rows, coef = exchange(dout, ddown, basis_t, *flat)
    place = jnp.stack([lax.axis_index("rep"), lax.axis_index("fsdp")]).astype(jnp.int32)
    wout, wdown, aout, adown, mout, mdown = finish(
        place, rows, coef.reshape(8, 64, WIDE), basis_t, *flat
    )
    return (
        jnp.transpose(wout, (0, 2, 1)),
        jnp.transpose(wdown, (0, 2, 1)),
        aout.reshape(anchor_out.shape),
        adown.reshape(anchor_down.shape),
        mout.reshape(moment_out.shape),
        mdown.reshape(moment_down.shape),
    )


def solution(mesh):
    return jax.shard_map(
        per_device,
        mesh=mesh,
        in_specs=(
            P("rep", None, "tp", "fsdp"),
            P("rep", None, "tp", "fsdp"),
            P(),
            P("rep", "tp", "fsdp", None),
            P("rep", "tp", "fsdp", None),
            P("rep", "tp", "fsdp", None),
            P("rep", "tp", "fsdp", None),
        ),
        out_specs=(
            P(None, "tp", "fsdp"),
            P(None, "tp", "fsdp"),
            P("rep", "tp", "fsdp", None),
            P("rep", "tp", "fsdp", None),
            P("rep", "tp", "fsdp", None),
            P("rep", "tp", "fsdp", None),
        ),
        check_vma=False,
    )
```
